32 devices in a mesh: beam: 2 (over x), chan: 8 (over z, y), tm: 2 (over core).
Axes of the slice: x: 2, y: 2, z: 4, core: 2. Of those that a mesh axis runs over, the one named last changes fastest.
Arguments:
- filterbank: bfloat16 [4096, 4096], P(('beam', 'chan'), 'tm'), parts along dimension 0, may hold values from -2500 to 2500
- local_delays: int32 [2048, 64], P('chan'), may hold values from 0 to 63
- lower_rows: int32 [3, 512], P(None, 'chan'), may hold values from 0 to 63
- upper_rows: int32 [3, 512], P(None, 'chan'), may hold values from 0 to 63
- level_shifts: int32 [3, 512], P(None, 'chan'), may hold values from 0 to 127, as said below
- box_widths: int32 [8], replicated, may hold values from 1 to 128, as said below
Outputs:
- snr: float32 [8, 1024, 4096], P(None, ('beam', 'chan'), 'tm'), parts along dimension 1
The draws below stay inside these ranges and needn't reach their ends.
There are 2 independent parts, one for each index of `beam`. The reference program is written for one: setup_inputs(seed, part) draws one part's arguments, and reference() takes and returns one part's arrays. A program takes and returns all parts, laid end to end along the dimension named above; an argument that names none is the same for every part. Nothing has to cross between parts.
Inputs may be any that keep to these rules, and one draw needn't show every extreme that they name: `level_shifts`: at level j every entry is below 64 * 2**j // 2, and that bound less one occurs at every level. `box_widths`: entry i lies in [2**i, 2**(i+1)) for i below 7; the last entry is 128.
All inputs are finite; a program needn't handle non-finite values.
Results may differ from the reference program's by a relative error of at most 0.0014.
Values may be sent and summed in bfloat16 or wider, within the bound.
A program may use at most 64 MiB of HBM per device.

```python
import math
import jax
import jax.numpy as jnp
from jax import lax

CH_DEV = 256
K = 64
DLOC = 64
NW = 8
XLEV = 3
WMAX = 128
CH = 2048
DMS = 512
TT = 4096
N_CHAN = 8


def draw_filterbank(key, part):
    key_gain = jax.random.fold_in(key, 11)
    key_noise = jax.random.fold_in(key, 12)
    moments = jnp.arange(TT, dtype=jnp.float32) / TT
    gains = jnp.exp(jax.random.uniform(key_gain, (CH, 1), minval=0.0, maxval=math.log(10.0)))
    envelope = jnp.exp(math.log(10.0) * moments)[None, :]
    noise = jnp.clip(jax.random.normal(key_noise, (CH, TT)), -6.0, 6.0)
    values = gains * envelope * noise
    return values.astype(jnp.bfloat16)


def draw_local_delays(key, part):
    key_values = jax.random.fold_in(key, 21)
    key_place = jax.random.fold_in(key, 22)
    values = jax.random.randint(key_values, (CH * K,), 0, DLOC)
    place = jax.random.randint(key_place, (), 0, CH * K)
    values = values.at[place].set(DLOC - 1)
    return values.reshape(CH, K).astype(jnp.int32)


def draw_level_shifts(key, part):
    layers = []
    for level in range(XLEV):
        bound = DLOC * 2 ** level // 2
        key_values = jax.random.fold_in(key, 100 + level)
        key_place = jax.random.fold_in(key, 200 + level)
        values = jax.random.randint(key_values, (DMS,), 0, bound)
        place = jax.random.randint(key_place, (), 0, DMS)
        layers.append(values.at[place].set(bound - 1))
    return jnp.stack(layers).astype(jnp.int32)


def draw_box_widths(key, part):
    lowest = 2 ** jnp.arange(NW, dtype=jnp.int32)
    extra = jax.random.randint(jax.random.fold_in(key, 31), (NW,), 0, 2 ** 20) % lowest
    widths = lowest + extra
    widths = widths.at[NW - 1].set(WMAX)
    return widths.astype(jnp.int32)


def set_ends(result, rng, low, largest):
    extent = result.shape
    spot = [jax.random.randint(jax.random.fold_in(rng, axis), (), 0, extent[axis]) for axis in range(len(extent))]
    result = result.at[tuple(spot)].set(low)
    longest = extent.index(max(extent))
    spot[longest] = (spot[longest] + 1) % extent[longest]
    return result.at[tuple(spot)].set(largest)


def setup_inputs(seed: int = 0, part: int = 0) -> dict:
    seeds = jax.random.split(jax.random.key(seed), 7)
    part_splits = jax.random.split(jax.random.fold_in(seeds[6], part), 7)
    filterbank = draw_filterbank(jax.random.fold_in(jax.random.fold_in(seeds[6], part), 71), part)
    local_delays = draw_local_delays(jax.random.fold_in(seeds[6], 71), part)
    lower_rows = set_ends(jax.random.randint(seeds[2], (XLEV, DMS), 0, K), jax.random.fold_in(seeds[2], 1), 0, K - 1).astype(jnp.int32)
    upper_rows = set_ends(jax.random.randint(seeds[3], (XLEV, DMS), 0, K), jax.random.fold_in(seeds[3], 1), 0, K - 1).astype(jnp.int32)
    level_shifts = draw_level_shifts(jax.random.fold_in(seeds[6], 71), part)
    box_widths = draw_box_widths(jax.random.fold_in(seeds[6], 71), part)
    return dict(filterbank=filterbank, local_delays=local_delays, lower_rows=lower_rows, upper_rows=upper_rows, level_shifts=level_shifts, box_widths=box_widths)


def delay_rows(series, shift_by, reach_now):
    length = series.shape[1]
    padded = jnp.pad(series, ((0, 0), (reach_now, 0)))

    def take_one(single, amount):
        return lax.dynamic_slice_in_dim(single, reach_now - amount, length, 0)
    return jax.vmap(take_one)(padded, shift_by)

def reference(filterbank, local_delays, lower_rows, upper_rows, level_shifts, box_widths):
    samples = filterbank.shape[1]
    channel_rows = filterbank.astype(jnp.float32).reshape(N_CHAN, CH_DEV, samples).transpose(1, 0, 2)
    channel_delays = local_delays.reshape(N_CHAN, CH_DEV, K).transpose(1, 0, 2)

    def block_series(single, amounts):
        padded = jnp.pad(single, (DLOC, 0))

        def take_one(amount):
            return lax.dynamic_slice_in_dim(padded, DLOC - amount, samples, 0)
        return jax.vmap(take_one)(amounts)

    def add_channel(summed, chan_item):
        rows_now, delays_now = chan_item
        return (summed + jax.vmap(block_series)(rows_now, delays_now), None)
    state, _ = lax.scan(add_channel, jnp.zeros((N_CHAN, K, samples), jnp.float32), (channel_rows, channel_delays))
    blocks = jnp.arange(N_CHAN, dtype=jnp.int32)
    for level in range(XLEV):
        bit_value = 2 ** level
        reach_now = DLOC * bit_value // 2
        low_block = blocks - (blocks & bit_value)
        high_block = low_block + bit_value
        low_index = lower_rows[level].reshape(N_CHAN, K)
        high_index = upper_rows[level].reshape(N_CHAN, K)
        shifts_now = level_shifts[level].reshape(N_CHAN * K)
        picked_low = state[low_block[:, None], low_index]
        picked_high = state[high_block[:, None], high_index].reshape(N_CHAN * K, samples)
        state = picked_low + delay_rows(picked_high, shifts_now, reach_now).reshape(N_CHAN, K, samples)
    series = state.reshape(N_CHAN * K, samples)
    mean_square = lax.optimization_barrier(jnp.mean(series * series, axis=1))
    inverse_rms = lax.rsqrt(mean_square + 1e-05)
    running = jnp.cumsum(jnp.pad(series, ((0, 0), (WMAX, 0))), axis=1)
    later_sum = running[:, WMAX:]

    def one_width(box_width):
        earlier = lax.dynamic_slice_in_dim(running, WMAX - box_width, samples, 1)
        return (later_sum - earlier) * inverse_rms[:, None] / jnp.sqrt(box_width.astype(jnp.float32))
    return lax.map(one_width, box_widths)
```

```python
import functools

import jax
import jax.numpy as jnp
from jax import lax
from jax.experimental import pallas as pl
from jax.experimental.pallas import tpu as pltpu
from jax.sharding import PartitionSpec as P

DLOC = 64
LANES = 128
FINE = 8
COARSE = DLOC // FINE


def lane_up(count):
    return -(-count // LANES) * LANES


def from_earlier(block, axis, distance):
    devices = range(lax.axis_size(axis))
    route = [(i - distance, i) for i in devices if i - distance in devices]
    return lax.ppermute(block, axis, route)


def from_partner(array, axis, distance):
    return lax.ppermute(array, axis, [(i, i ^ 1 << distance) for i in range(lax.axis_size(axis))])


def left_context(block, axis, width):
    samples = block.shape[1]
    pieces = []
    distance = 1
    while width > 0:
        part = min(width, samples)
        if distance < lax.axis_size(axis):
            pieces.insert(0, from_earlier(block[:, samples - part :], axis, distance))
        else:
            pieces.insert(0, jnp.zeros((block.shape[0], width), block.dtype))
            part = width
        width -= part
        distance += 1
    return pieces[0] if len(pieces) == 1 else jnp.concatenate(pieces, axis=1)


def code_rows(rows):
    largest = jnp.maximum(jnp.max(jnp.abs(rows), axis=1, keepdims=True), 2.0**-100)
    exponent = jnp.floor(jnp.log2(largest))
    coded = jnp.round(jnp.clip(rows * jnp.exp2(14.0 - exponent), -32767.0, 32767.0))
    column = lax.broadcasted_iota(jnp.int32, rows.shape, 1)
    return jnp.where(column == 0, exponent, coded).astype(jnp.int32).astype(jnp.int16)


def decode_rows(coded):
    values = coded.astype(jnp.int32).astype(jnp.float32)
    return values * jnp.exp2(values[:, :1] - 14.0)


def dedisperse_kernel(tile, rim_ref, fb_ref, delays_ref, own_ref, coded_ref, ext, onehot, spread, partial):
    channels, samples = fb_ref.shape
    rows = delays_ref.shape[0]
    rim = rim_ref.shape[1]
    total = rim + samples
    ext[:, :LANES] = jnp.zeros((channels, LANES), jnp.bfloat16)
    ext[:, LANES : LANES + rim] = rim_ref[...]
    ext[:, LANES + rim :] = fb_ref[...]
    for coarse in range(COARSE):
        relative = delays_ref[...] - FINE * coarse
        for fine in range(FINE):
            onehot[coarse * rows : (coarse + 1) * rows, fine * channels : (fine + 1) * channels] = (
                jnp.where(relative == fine, 1.0, 0.0).astype(jnp.bfloat16)
            )

    def step(index, carry):
        start = pl.multiple_of(index * tile, LANES)
        window = ext[:, pl.ds(start, tile + LANES)]
        for fine in range(FINE):
            spread[fine * channels : (fine + 1) * channels, :] = window[
                :, LANES - fine : LANES - fine + tile
            ]
        partial[:, pl.ds(start, tile)] = jnp.dot(
            onehot[...], spread[...], preferred_element_type=jnp.float32
        )
        return carry

    lax.fori_loop(0, total // tile, step, 0)
    width = own_ref.shape[1]
    summed = partial[:rows, total - width :]
    for coarse in range(1, COARSE):
        back = total - width - FINE * coarse
        summed = summed + partial[coarse * rows : (coarse + 1) * rows, back : back + width]
    own_ref[...] = summed
    coded_ref[...] = code_rows(summed)


def dedisperse(rim, filterbank, delays, width):
    channels, samples = filterbank.shape
    rows = delays.shape[0]
    total = rim.shape[1] + samples
    tile = max(t for t in (512, 256, 128) if total % t == 0)
    return pl.pallas_call(
        functools.partial(dedisperse_kernel, tile),
        name="dedisperse",
        out_shape=(
            jax.ShapeDtypeStruct((rows, width), jnp.float32),
            jax.ShapeDtypeStruct((rows, width), jnp.int16),
        ),
        scratch_shapes=[
            pltpu.VMEM((channels, LANES + total), jnp.bfloat16),
            pltpu.VMEM((COARSE * rows, FINE * channels), jnp.bfloat16),
            pltpu.VMEM((FINE * channels, tile), jnp.bfloat16),
            pltpu.VMEM((COARSE * rows, total), jnp.float32),
        ],
        compiler_params=pltpu.CompilerParams(vmem_limit_bytes=40 * 2**20),
    )(rim, filterbank, delays)


def pick(index, source):
    rows = source.shape[0]
    chosen = jnp.where(
        lax.broadcasted_iota(jnp.int32, (index.shape[0], 2 * rows), 1) % rows == index, 1.0, 0.0
    ).astype(jnp.bfloat16)
    high = source.astype(jnp.bfloat16)
    low = (source - high.astype(jnp.float32)).astype(jnp.bfloat16)
    return jnp.dot(
        chosen, jnp.concatenate([high, low], axis=0), preferred_element_type=jnp.float32
    )


def merge_kernel(level, levels, side_ref, own_ref, coded_ref, plan_ref, *out_refs):
    reach = DLOC * 2**level // 2
    own = own_ref[...]
    partner = decode_rows(coded_ref[...])
    upper_side = side_ref[0] == 1
    low_source = jnp.where(upper_side, partner, own)
    high_source = jnp.where(upper_side, own, partner)
    plan = plan_ref[...]
    low = pick(plan[:, level : level + 1], low_source)
    high = pick(plan[:, levels + level : levels + level + 1], high_source)
    shift = plan[:, 2 * levels + level : 2 * levels + level + 1]
    for bit in range((reach - 1).bit_length()):
        high = jnp.where((shift >> bit) & 1 == 1, pltpu.roll(high, 2**bit, 1), high)
    column = lax.broadcasted_iota(jnp.int32, high.shape, 1)
    merged = low + jnp.where(column < shift, 0.0, high)
    width = out_refs[0].shape[1]
    merged = merged[:, merged.shape[1] - width :]
    out_refs[0][...] = merged
    if level < levels - 1:
        out_refs[1][...] = code_rows(merged)
    else:
        fresh = merged[:, LANES:]
        out_refs[1][...] = jnp.sum(fresh * fresh, axis=1, keepdims=True)


def merge(level, levels, side, own, coded, plan, width):
    rows = own.shape[0]
    second = (
        jax.ShapeDtypeStruct((rows, width), jnp.int16)
        if level < levels - 1
        else jax.ShapeDtypeStruct((rows, 1), jnp.float32)
    )
    vmem = pl.BlockSpec(memory_space=pltpu.VMEM)
    return pl.pallas_call(
        functools.partial(merge_kernel, level, levels),
        name=f"merge_{level}",
        out_shape=(jax.ShapeDtypeStruct((rows, width), jnp.float32), second),
        in_specs=[pl.BlockSpec(memory_space=pltpu.SMEM), vmem, vmem, vmem],
        out_specs=(vmem, vmem),
        compiler_params=pltpu.CompilerParams(vmem_limit_bytes=32 * 2**20),
    )(side, own, coded, plan)


def box_kernel(times, widths_ref, state_ref, squares_ref, out_ref, stacked):
    rows = state_ref.shape[0]
    tiles = out_ref.shape[2] // LANES
    per_step = out_ref.shape[0]

    @pl.when(pl.program_id(0) == 0)
    def _():
        for tile in range(tiles):
            part = state_ref[:, tile * LANES : (tile + 2) * LANES]
            high = part.astype(jnp.bfloat16)
            low = (part - high.astype(jnp.float32)).astype(jnp.bfloat16)
            stacked[tile * rows : (tile + 1) * rows, : 2 * LANES] = high
            stacked[tile * rows : (tile + 1) * rows, 2 * LANES :] = low

    inverse = lax.rsqrt(squares_ref[...] / times + 1e-05)
    masks = []
    factors = []
    for which in range(per_step):
        box_width = widths_ref[pl.program_id(0) * per_step + which]
        at = lax.broadcasted_iota(jnp.int32, (2 * LANES, LANES), 0) - LANES
        to = lax.broadcasted_iota(jnp.int32, (2 * LANES, LANES), 1)
        inside = (at <= to) & (at > to - box_width)
        mask = jnp.where(inside, 1.0, 0.0).astype(jnp.bfloat16)
        masks.append(jnp.concatenate([mask, mask], axis=0))
        root = jnp.sqrt(jnp.full((rows, LANES), box_width.astype(jnp.float32)))
        factors.append(inverse / root)
    boxes = jnp.dot(
        stacked[...], jnp.concatenate(masks, axis=1), preferred_element_type=jnp.float32
    )
    for which in range(per_step):
        for tile in range(tiles):
            out_ref[which, :, tile * LANES : (tile + 1) * LANES] = (
                boxes[tile * rows : (tile + 1) * rows, which * LANES : (which + 1) * LANES]
                * factors[which]
            )


def box_filter(widths, state, squares, samples, times):
    rows = state.shape[0]
    count = widths.shape[0]
    per_step = 2 if count % 2 == 0 else 1
    return pl.pallas_call(
        functools.partial(box_kernel, times),
        name="boxes",
        grid=(count // per_step,),
        out_shape=jax.ShapeDtypeStruct((count, rows, samples), jnp.float32),
        in_specs=[
            pl.BlockSpec(memory_space=pltpu.SMEM),
            pl.BlockSpec(memory_space=pltpu.VMEM),
            pl.BlockSpec(memory_space=pltpu.VMEM),
        ],
        out_specs=pl.BlockSpec((per_step, rows, samples), lambda i: (i, 0, 0)),
        scratch_shapes=[pltpu.VMEM((samples // LANES * rows, 4 * LANES), jnp.bfloat16)],
        compiler_params=pltpu.CompilerParams(vmem_limit_bytes=32 * 2**20),
    )(widths, state, squares)


def local(filterbank, local_delays, lower_rows, upper_rows, level_shifts, box_widths):
    samples = filterbank.shape[1]
    levels = lax.axis_size("chan").bit_length() - 1
    needs = [LANES]
    for level in reversed(range(levels)):
        needs.insert(0, needs[0] - (level == levels - 1) + DLOC * 2**level // 2 - 1)
    widths = [samples + lane_up(need + 1) for need in needs[:-1]] + [samples + LANES]
    rim = left_context(filterbank, "tm", lane_up(widths[0] - samples + DLOC - 1))
    plan = jnp.concatenate([lower_rows, upper_rows, level_shifts], axis=0).T
    own, coded = dedisperse(rim, filterbank, local_delays.T, widths[0])
    for level in range(levels):
        side = (lax.axis_index("chan") >> level & 1).astype(jnp.int32)[None]
        partner = from_partner(coded, "chan", level)
        own, coded = merge(level, levels, side, own, partner, plan, widths[level + 1])
    squares = lax.psum(coded, "tm")
    return box_filter(box_widths, own, squares, samples, samples * lax.axis_size("tm"))


def solution(mesh):
    placed = (
        P(("beam", "chan"), "tm"),
        P("chan", None),
        P(None, "chan"),
        P(None, "chan"),
        P(None, "chan"),
        P(),
    )
    return jax.shard_map(
        local,
        mesh=mesh,
        in_specs=placed,
        out_specs=P(None, ("beam", "chan"), "tm"),
        check_vma=False,
    )
```

```python
import functools

import jax
import jax.numpy as jnp
from jax import lax
from jax.experimental import pallas as pl
from jax.experimental.pallas import tpu as pltpu
from jax.sharding import PartitionSpec as P

DLOC = 64
LANES = 128
FINE = 8
COARSE = DLOC // FINE
CHUNKS = 3
MESH = pl.DeviceIdType.MESH


def lane_up(count):
    return -(-count // LANES) * LANES


def code_rows(rows, lead):
    largest = jnp.maximum(jnp.max(jnp.abs(rows), axis=1, keepdims=True), 2.0**-100)
    exponent = jnp.floor(jnp.log2(largest))
    coded = jnp.round(jnp.clip(rows * jnp.exp2(14.0 - exponent), -32767.0, 32767.0))
    if lead:
        front = jnp.broadcast_to(exponent, (rows.shape[0], lead))
        coded = jnp.concatenate([front, coded], axis=1)
    else:
        column = lax.broadcasted_iota(jnp.int32, rows.shape, 1)
        coded = jnp.where(column == 0, exponent, coded)
    return coded.astype(jnp.int32).astype(jnp.int16)


def decode_rows(coded, lead):
    values = coded.astype(jnp.int32).astype(jnp.float32)
    return values[:, lead:] * jnp.exp2(values[:, :1] - 14.0)


def as_column(row):
    count = row.shape[1]
    at = lax.broadcasted_iota(jnp.int32, (count, count), 0)
    to = lax.broadcasted_iota(jnp.int32, (count, count), 1)
    spread = jnp.where(at == to, row.astype(jnp.float32), 0.0)
    return jnp.sum(spread, axis=1, keepdims=True).astype(jnp.int32)


def pick(index, source):
    rows = source.shape[0]
    at = lax.broadcasted_iota(jnp.int32, (index.shape[0], rows), 1)
    once = jnp.where(at == index, 1.0, 0.0).astype(jnp.bfloat16)
    chosen = jnp.concatenate([once, once], axis=1)
    high = source.astype(jnp.bfloat16)
    low = (source - high.astype(jnp.float32)).astype(jnp.bfloat16)
    return jnp.dot(
        chosen, jnp.concatenate([high, low], axis=0), preferred_element_type=jnp.float32
    )


def sweep_kernel(
    edges,
    starts,
    rim,
    fb_ref,
    delays_ref,
    lower_ref,
    upper_ref,
    shifts_ref,
    state_ref,
    squares_ref,
    ext,
    onehot,
    spread,
    partial,
    owns,
    picked,
    outgoing,
    incoming,
    square_out,
    square_in,
    local_sem,
    pair_send,
    pair_recv,
    send_sem,
    recv_sem,
):
    channels, samples = fb_ref.shape
    rows = delays_ref.shape[0]
    levels = len(owns)
    chunks = len(edges) - 1
    width = edges[-1]
    total = rim + samples
    skip = total - width
    tail = picked[0].shape[1] - width
    sent_rim = min(rim, samples)
    empty = LANES + rim - sent_rim

    chan = lax.axis_index("chan")
    tm = lax.axis_index("tm")
    sides = [lax.rem(lax.div(chan, 1 << level), 2) for level in range(levels)]
    partners = [
        {"chan": chan + (1 << level) - (2 << level) * sides[level]} for level in range(levels)
    ]
    pair = {"tm": 1 - tm}

    barrier = pltpu.get_barrier_semaphore()
    for device in [pair] + partners:
        pl.semaphore_signal(barrier, inc=1, device_id=device, device_id_type=MESH)
    own_copy = pltpu.make_async_copy(fb_ref, ext.at[:, pl.ds(LANES + rim, samples)], local_sem)
    own_copy.start()
    pl.semaphore_wait(barrier, levels + 1)
    rim_copy = pltpu.make_async_remote_copy(
        src_ref=fb_ref.at[:, pl.ds(samples - sent_rim, sent_rim)],
        dst_ref=ext.at[:, pl.ds(empty, sent_rim)],
        send_sem=pair_send.at[0],
        recv_sem=pair_recv.at[0],
        device_id=pair,
        device_id_type=MESH,
    )
    rim_copy.start()

    ext[:, :empty] = jnp.zeros((channels, empty), jnp.bfloat16)
    for level in range(levels):
        picked[level][:, :tail] = jnp.zeros((rows, tail), jnp.float32)
    for coarse in range(COARSE):
        relative = delays_ref[...] - FINE * coarse
        for fine in range(FINE):
            onehot[coarse * rows : (coarse + 1) * rows, fine * channels : (fine + 1) * channels] = (
                jnp.where(relative == fine, 1.0, 0.0).astype(jnp.bfloat16)
            )
    lows = [as_column(lower_ref[level : level + 1, :]) for level in range(levels)]
    highs = [as_column(upper_ref[level : level + 1, :]) for level in range(levels)]
    shifts = [as_column(shifts_ref[level : level + 1, :]) for level in range(levels)]

    def exchange(level, chunk):
        return pltpu.make_async_remote_copy(
            src_ref=outgoing[level][chunk],
            dst_ref=incoming[level][chunk],
            send_sem=send_sem.at[level, chunk],
            recv_sem=recv_sem.at[level, chunk],
            device_id=partners[level],
            device_id_type=MESH,
        )

    def lead(chunk):
        return LANES if chunk else 0

    def first_of(level, chunk):
        return max(edges[chunk], starts[level])

    def hand_on(level, chunk, values):
        owns[level][:, first_of(level, chunk) : edges[chunk + 1]] = values
        outgoing[level][chunk][...] = code_rows(values, lead(chunk))
        exchange(level, chunk).start()

    def dedisperse(chunk):
        begin = skip + edges[chunk] if chunk else 0
        end = skip + edges[chunk + 1]
        tile = 2 * LANES if (end - begin) % (2 * LANES) == 0 else LANES

        def step(index, carry):
            start = pl.multiple_of(begin + index * tile, LANES)
            window = ext[:, pl.ds(start, tile + LANES)]
            for fine in range(FINE):
                spread[fine * channels : (fine + 1) * channels, :tile] = window[
                    :, LANES - fine : LANES - fine + tile
                ]
            partial[:, pl.ds(start, tile)] = jnp.dot(
                onehot[...], spread[:, :tile], preferred_element_type=jnp.float32
            )
            return carry

        lax.fori_loop(0, (end - begin) // tile, step, 0)
        summed = None
        for coarse in range(COARSE):
            back = skip - FINE * coarse
            term = partial[
                coarse * rows : (coarse + 1) * rows, back + edges[chunk] : back + edges[chunk + 1]
            ]
            summed = term if summed is None else summed + term
        hand_on(0, chunk, summed)

    def merge(level, chunk):
        begin, end = first_of(level, chunk), edges[chunk + 1]
        exchange(level, chunk).wait_recv()
        own = owns[level][:, begin:end]
        partner = decode_rows(incoming[level][chunk][...], lead(chunk))
        upper_side = sides[level] == 1
        low = pick(lows[level], jnp.where(upper_side, partner, own))
        high = pick(highs[level], jnp.where(upper_side, own, partner))
        reach = DLOC * 2**level // 2
        room = lane_up(reach)
        picked[level][:, tail + begin : tail + end] = high
        moved = picked[level][:, tail + begin - room : tail + end]
        for bit in range((reach - 1).bit_length()):
            moved = jnp.where(
                (shifts[level] >> bit) & 1 == 1, pltpu.roll(moved, 2**bit, 1), moved
            )
        after = max(edges[chunk], starts[level + 1])
        return (low + moved[:, room:])[:, after - begin :]

    own_copy.wait()
    rim_copy.wait()
    ext[:, empty : LANES + rim] = jnp.where(
        tm == 0, jnp.zeros((channels, sent_rim), jnp.bfloat16), ext[:, empty : LANES + rim]
    )
    squares = jnp.zeros((rows, 1), jnp.float32)
    for turn in range(chunks + levels):
        if turn < chunks:
            dedisperse(turn)
        for level in range(levels):
            chunk = turn - 1 - level
            if not 0 <= chunk < chunks:
                continue
            merged = merge(level, chunk)
            if level < levels - 1:
                hand_on(level + 1, chunk, merged)
            else:
                begin = first_of(levels, chunk)
                state_ref[:, begin - starts[levels] : edges[chunk + 1] - starts[levels]] = merged
                if edges[chunk + 1] > width - samples:
                    fresh = merged[:, max(width - samples - begin, 0) :]
                    squares = squares + jnp.sum(fresh * fresh, axis=1, keepdims=True)
    square_out[...] = jnp.broadcast_to(squares, (rows, LANES))
    square_copy = pltpu.make_async_remote_copy(
        src_ref=square_out,
        dst_ref=square_in,
        send_sem=pair_send.at[1],
        recv_sem=pair_recv.at[1],
        device_id=pair,
        device_id_type=MESH,
    )
    square_copy.start()
    for level in range(levels):
        for chunk in range(chunks):
            exchange(level, chunk).wait_send()
    square_copy.wait()
    squares_ref[...] = square_out[...] + square_in[...]


def sweep(filterbank, delays, lower_rows, upper_rows, level_shifts, widths):
    channels, samples = filterbank.shape
    rows = delays.shape[0]
    levels = len(widths) - 1
    width = widths[0]
    rim = lane_up(width - samples + DLOC - 1)
    total = rim + samples
    starts = [width - each for each in widths]
    tiles = width // LANES
    fair = (tiles - 1) // CHUNKS
    most = (widths[-1] // LANES - 1) // max(CHUNKS - 1, 1)
    later = min(fair, most) // 2 * 2 or 1
    sizes = [tiles - later * (CHUNKS - 1)] + [later] * (CHUNKS - 1)
    edges = [LANES * sum(sizes[:count]) for count in range(CHUNKS + 1)]

    def coded():
        return [
            [
                pltpu.VMEM(
                    (rows, edges[c + 1] - max(edges[c], starts[j]) + (LANES if c else 0)),
                    jnp.int16,
                )
                for c in range(CHUNKS)
            ]
            for j in range(levels)
        ]

    tail = lane_up(DLOC * 2 ** (levels - 1) // 2)
    vmem = pl.BlockSpec(memory_space=pltpu.VMEM)
    return pl.pallas_call(
        functools.partial(sweep_kernel, edges, starts, rim),
        name="sweep",
        out_shape=(
            jax.ShapeDtypeStruct((rows, widths[-1]), jnp.float32),
            jax.ShapeDtypeStruct((rows, LANES), jnp.float32),
        ),
        in_specs=[pl.BlockSpec(memory_space=pltpu.HBM), vmem, vmem, vmem, vmem],
        out_specs=(vmem, vmem),
        scratch_shapes=[
            pltpu.VMEM((channels, LANES + total), jnp.bfloat16),
            pltpu.VMEM((COARSE * rows, FINE * channels), jnp.bfloat16),
            pltpu.VMEM((FINE * channels, 2 * LANES), jnp.bfloat16),
            pltpu.VMEM((COARSE * rows, total), jnp.float32),
            [pltpu.VMEM((rows, width), jnp.float32) for _ in range(levels)],
            [pltpu.VMEM((rows, tail + width), jnp.float32) for _ in range(levels)],
            coded(),
            coded(),
            pltpu.VMEM((rows, LANES), jnp.float32),
            pltpu.VMEM((rows, LANES), jnp.float32),
            pltpu.SemaphoreType.DMA,
            pltpu.SemaphoreType.DMA((2,)),
            pltpu.SemaphoreType.DMA((2,)),
            pltpu.SemaphoreType.DMA((levels, CHUNKS)),
            pltpu.SemaphoreType.DMA((levels, CHUNKS)),
        ],
        compiler_params=pltpu.CompilerParams(
            collective_id=0, has_side_effects=True, vmem_limit_bytes=48 * 2**20
        ),
    )(filterbank, delays, lower_rows, upper_rows, level_shifts)


def box_kernel(times, widths_ref, state_ref, squares_ref, out_ref, stacked):
    rows = state_ref.shape[0]
    tiles = out_ref.shape[2] // LANES
    per_step = out_ref.shape[0]

    @pl.when(pl.program_id(0) == 0)
    def _():
        for tile in range(tiles):
            part = state_ref[:, tile * LANES : (tile + 2) * LANES]
            high = part.astype(jnp.bfloat16)
            low = (part - high.astype(jnp.float32)).astype(jnp.bfloat16)
            stacked[tile * rows : (tile + 1) * rows, : 2 * LANES] = high
            stacked[tile * rows : (tile + 1) * rows, 2 * LANES :] = low

    inverse = lax.rsqrt(squares_ref[...] / times + 1e-05)
    masks = []
    factors = []
    for which in range(per_step):
        box_width = widths_ref[pl.program_id(0) * per_step + which]
        at = lax.broadcasted_iota(jnp.int32, (2 * LANES, LANES), 0) - LANES
        to = lax.broadcasted_iota(jnp.int32, (2 * LANES, LANES), 1)
        inside = (at <= to) & (at > to - box_width)
        mask = jnp.where(inside, 1.0, 0.0).astype(jnp.bfloat16)
        masks.append(jnp.concatenate([mask, mask], axis=0))
        root = jnp.sqrt(jnp.full((rows, LANES), box_width.astype(jnp.float32)))
        factors.append(inverse / root)
    boxes = jnp.dot(
        stacked[...], jnp.concatenate(masks, axis=1), preferred_element_type=jnp.float32
    )
    for which in range(per_step):
        for tile in range(tiles):
            out_ref[which, :, tile * LANES : (tile + 1) * LANES] = (
                boxes[tile * rows : (tile + 1) * rows, which * LANES : (which + 1) * LANES]
                * factors[which]
            )


def box_filter(widths, state, squares, samples, times):
    rows = state.shape[0]
    count = widths.shape[0]
    per_step = 2 if count % 2 == 0 else 1
    return pl.pallas_call(
        functools.partial(box_kernel, times),
        name="boxes",
        grid=(count // per_step,),
        out_shape=jax.ShapeDtypeStruct((count, rows, samples), jnp.float32),
        in_specs=[
            pl.BlockSpec(memory_space=pltpu.SMEM),
            pl.BlockSpec(memory_space=pltpu.VMEM),
            pl.BlockSpec(memory_space=pltpu.VMEM),
        ],
        out_specs=pl.BlockSpec((per_step, rows, samples), lambda i: (i, 0, 0)),
        scratch_shapes=[pltpu.VMEM((samples // LANES * rows, 4 * LANES), jnp.bfloat16)],
        compiler_params=pltpu.CompilerParams(vmem_limit_bytes=32 * 2**20),
    )(widths, state, squares)


def local(filterbank, local_delays, lower_rows, upper_rows, level_shifts, box_widths):
    samples = filterbank.shape[1]
    levels = lax.axis_size("chan").bit_length() - 1
    needs = [LANES]
    for level in reversed(range(levels)):
        needs.insert(0, needs[0] - (level == levels - 1) + DLOC * 2**level // 2 - 1)
    widths = [samples + lane_up(need + 1) for need in needs[:-1]] + [samples + LANES]
    state, squares = sweep(
        filterbank, local_delays.T, lower_rows, upper_rows, level_shifts, widths
    )
    return box_filter(box_widths, state, squares, samples, samples * lax.axis_size("tm"))


def solution(mesh):
    placed = (
        P(("beam", "chan"), "tm"),
        P("chan", None),
        P(None, "chan"),
        P(None, "chan"),
        P(None, "chan"),
        P(),
    )
    return jax.shard_map(
        local,
        mesh=mesh,
        in_specs=placed,
        out_specs=P(None, ("beam", "chan"), "tm"),
        check_vma=False,
    )
```

```python
import functools

import jax
import jax.numpy as jnp
from jax import lax
from jax.experimental import pallas as pl
from jax.experimental.pallas import tpu as pltpu
from jax.sharding import PartitionSpec as P

DLOC = 64
LANES = 128
FINE = 8
COARSE = DLOC // FINE
CHUNKS = 3
PACKED = 16
MESH = pl.DeviceIdType.MESH


def lane_up(count):
    return -(-count // LANES) * LANES


def code_rows(rows):
    largest = jnp.maximum(jnp.max(jnp.abs(rows), axis=1, keepdims=True), 2.0**-100)
    exponent = jnp.floor(jnp.log2(largest))
    coded = jnp.round(jnp.clip(rows * jnp.exp2(14.0 - exponent), -32767.0, 32767.0))
    at = lax.broadcasted_iota(jnp.int32, (rows.shape[0], LANES), 0)
    to = lax.broadcasted_iota(jnp.int32, (rows.shape[0], LANES), 1)
    along = jnp.sum(jnp.where(at == to, exponent, 0.0), axis=0, keepdims=True)
    along = jnp.broadcast_to(along, (PACKED, LANES))
    return coded.astype(jnp.int32).astype(jnp.int16), along.astype(jnp.int32).astype(jnp.int16)


def decode_rows(coded, along):
    values = coded.astype(jnp.int32).astype(jnp.float32)
    exponents = along.astype(jnp.int32)[:1, : coded.shape[0]]
    return values * jnp.exp2(as_column(exponents).astype(jnp.float32) - 14.0)


def as_column(row):
    count = row.shape[1]
    at = lax.broadcasted_iota(jnp.int32, (count, count), 0)
    to = lax.broadcasted_iota(jnp.int32, (count, count), 1)
    spread = jnp.where(at == to, row.astype(jnp.float32), 0.0)
    return jnp.sum(spread, axis=1, keepdims=True).astype(jnp.int32)


def pick(index, source):
    rows = source.shape[0]
    at = lax.broadcasted_iota(jnp.int32, (index.shape[0], rows), 1)
    once = jnp.where(at == index, 1.0, 0.0).astype(jnp.bfloat16)
    chosen = jnp.concatenate([once, once], axis=1)
    high = source.astype(jnp.bfloat16)
    low = (source - high.astype(jnp.float32)).astype(jnp.bfloat16)
    return jnp.dot(
        chosen, jnp.concatenate([high, low], axis=0), preferred_element_type=jnp.float32
    )


def sweep_kernel(
    edges,
    starts,
    rim,
    fb_ref,
    delays_hbm,
    lower_hbm,
    upper_hbm,
    shifts_hbm,
    widths_hbm,
    state_ref,
    squares_ref,
    widths_ref,
    delays_ref,
    lower_ref,
    upper_ref,
    shifts_ref,
    widths_row,
    ext,
    onehot,
    spread,
    partial,
    owns,
    picked,
    outgoing,
    incoming,
    scale_out,
    scale_in,
    square_out,
    square_in,
    local_sem,
    small_sem,
    pair_send,
    pair_recv,
    send_sem,
    recv_sem,
    scale_send,
    scale_recv,
):
    channels, samples = fb_ref.shape
    rows = delays_ref.shape[0]
    levels = len(owns)
    chunks = len(edges) - 1
    width = edges[-1]
    total = rim + samples
    skip = total - width
    tail = picked[0].shape[1] - width
    sent_rim = min(rim, samples)
    empty = LANES + rim - sent_rim

    chan = lax.axis_index("chan")
    tm = lax.axis_index("tm")
    sides = [lax.rem(lax.div(chan, 1 << level), 2) for level in range(levels)]
    partners = [
        {"chan": chan + (1 << level) - (2 << level) * sides[level]} for level in range(levels)
    ]
    pair = {"tm": 1 - tm}

    barrier = pltpu.get_barrier_semaphore()
    for device in [pair] + partners:
        pl.semaphore_signal(barrier, inc=1, device_id=device, device_id_type=MESH)
    own_copy = pltpu.make_async_copy(fb_ref, ext.at[:, pl.ds(LANES + rim, samples)], local_sem)
    small_copies = [
        pltpu.make_async_copy(source, target, small_sem.at[at])
        for at, (source, target) in enumerate(
            [
                (delays_hbm, delays_ref),
                (lower_hbm, lower_ref),
                (upper_hbm, upper_ref),
                (shifts_hbm, shifts_ref),
                (widths_hbm, widths_row),
            ]
        )
    ]
    for copy in small_copies:
        copy.start()
    own_copy.start()
    pl.semaphore_wait(barrier, levels + 1)
    rim_copy = pltpu.make_async_remote_copy(
        src_ref=fb_ref.at[:, pl.ds(samples - sent_rim, sent_rim)],
        dst_ref=ext.at[:, pl.ds(empty, sent_rim)],
        send_sem=pair_send.at[0],
        recv_sem=pair_recv.at[0],
        device_id=pair,
        device_id_type=MESH,
    )
    rim_copy.start()

    ext[:, :empty] = jnp.zeros((channels, empty), jnp.bfloat16)
    for level in range(levels):
        picked[level][:, :tail] = jnp.zeros((rows, tail), jnp.float32)
    for copy in small_copies:
        copy.wait()
    widths_ref[...] = jnp.broadcast_to(as_column(widths_row[...]), widths_ref.shape)
    for coarse in range(COARSE):
        relative = delays_ref[...] - FINE * coarse
        for fine in range(FINE):
            onehot[coarse * rows : (coarse + 1) * rows, fine * channels : (fine + 1) * channels] = (
                jnp.where(relative == fine, 1.0, 0.0).astype(jnp.bfloat16)
            )
    lows = [as_column(lower_ref[level : level + 1, :]) for level in range(levels)]
    highs = [as_column(upper_ref[level : level + 1, :]) for level in range(levels)]
    shifts = [as_column(shifts_ref[level : level + 1, :]) for level in range(levels)]

    def first_of(level, chunk):
        return max(edges[chunk], starts[level])

    def history(level, chunk):
        begin = first_of(level, chunk)
        return min(max(width - samples - begin, 0), edges[chunk + 1] - begin)

    def exchange(level, chunk, act):
        old = history(level, chunk)
        size = edges[chunk + 1] - first_of(level, chunk)

        def columns(begin):
            act(
                pltpu.make_async_remote_copy(
                    src_ref=outgoing[level][chunk].at[:, pl.ds(begin, size - begin)],
                    dst_ref=incoming[level][chunk].at[:, pl.ds(begin, size - begin)],
                    send_sem=send_sem.at[level, chunk],
                    recv_sem=recv_sem.at[level, chunk],
                    device_id=partners[level],
                    device_id_type=MESH,
                )
            )

        act(
            pltpu.make_async_remote_copy(
                src_ref=scale_out.at[level, chunk],
                dst_ref=scale_in.at[level, chunk],
                send_sem=scale_send.at[level, chunk],
                recv_sem=scale_recv.at[level, chunk],
                device_id=partners[level],
                device_id_type=MESH,
            )
        )
        if old:
            pl.when(tm > 0)(lambda: columns(0))
            if old < size:
                pl.when(tm == 0)(lambda: columns(old))
        else:
            columns(0)

    def hand_on(level, chunk, values):
        owns[level][:, first_of(level, chunk) : edges[chunk + 1]] = values
        outgoing[level][chunk][...], scale_out[level, chunk] = code_rows(values)
        exchange(level, chunk, lambda copy: copy.start())

    @pl.when(tm == 0)
    def _():
        for level in range(levels):
            for chunk in range(chunks):
                old = history(level, chunk)
                if old:
                    incoming[level][chunk][:, :old] = jnp.zeros((rows, old), jnp.int16)

    def dedisperse(chunk):
        begin = skip + edges[chunk] if chunk else 0
        end = skip + edges[chunk + 1]
        tile = 2 * LANES if (end - begin) % (2 * LANES) == 0 else LANES

        def step(index, carry):
            start = pl.multiple_of(begin + index * tile, LANES)
            window = ext[:, pl.ds(start, tile + LANES)]
            for fine in range(FINE):
                spread[fine * channels : (fine + 1) * channels, :tile] = window[
                    :, LANES - fine : LANES - fine + tile
                ]
            partial[:, pl.ds(start, tile)] = jnp.dot(
                onehot[...], spread[:, :tile], preferred_element_type=jnp.float32
            )
            return carry

        lax.fori_loop(0, (end - begin) // tile, step, 0)
        summed = None
        for coarse in range(COARSE):
            back = skip - FINE * coarse
            term = partial[
                coarse * rows : (coarse + 1) * rows, back + edges[chunk] : back + edges[chunk + 1]
            ]
            summed = term if summed is None else summed + term
        hand_on(0, chunk, summed)

    def merge(level, chunk):
        begin, end = first_of(level, chunk), edges[chunk + 1]
        exchange(level, chunk, lambda copy: copy.wait_recv())
        own = owns[level][:, begin:end]
        partner = decode_rows(incoming[level][chunk][...], scale_in[level, chunk])
        upper_side = sides[level] == 1
        low = pick(lows[level], jnp.where(upper_side, partner, own))
        high = pick(highs[level], jnp.where(upper_side, own, partner))
        reach = DLOC * 2**level // 2
        room = lane_up(reach)
        picked[level][:, tail + begin : tail + end] = high
        moved = picked[level][:, tail + begin - room : tail + end]
        for bit in range((reach - 1).bit_length()):
            moved = jnp.where(
                (shifts[level] >> bit) & 1 == 1, pltpu.roll(moved, 2**bit, 1), moved
            )
        after = max(edges[chunk], starts[level + 1])
        return (low + moved[:, room:])[:, after - begin :]

    own_copy.wait()
    rim_copy.wait()
    ext[:, empty : LANES + rim] = jnp.where(
        tm == 0, jnp.zeros((channels, sent_rim), jnp.bfloat16), ext[:, empty : LANES + rim]
    )
    squares = jnp.zeros((rows, 1), jnp.float32)
    for turn in range(chunks + levels):
        if turn < chunks:
            dedisperse(turn)
        for level in range(levels):
            chunk = turn - 1 - level
            if not 0 <= chunk < chunks:
                continue
            merged = merge(level, chunk)
            if level < levels - 1:
                hand_on(level + 1, chunk, merged)
            else:
                begin = first_of(levels, chunk)
                state_ref[:, begin - starts[levels] : edges[chunk + 1] - starts[levels]] = merged
                if edges[chunk + 1] > width - samples:
                    fresh = merged[:, max(width - samples - begin, 0) :]
                    squares = squares + jnp.sum(fresh * fresh, axis=1, keepdims=True)
    square_out[...] = jnp.broadcast_to(squares, (rows, LANES))
    square_copy = pltpu.make_async_remote_copy(
        src_ref=square_out,
        dst_ref=square_in,
        send_sem=pair_send.at[1],
        recv_sem=pair_recv.at[1],
        device_id=pair,
        device_id_type=MESH,
    )
    square_copy.start()
    for level in range(levels):
        for chunk in range(chunks):
            exchange(level, chunk, lambda copy: copy.wait_send())
    square_copy.wait()
    squares_ref[...] = square_out[...] + square_in[...]


def sweep(filterbank, delays, lower_rows, upper_rows, level_shifts, box_widths, widths):
    channels, samples = filterbank.shape
    rows = delays.shape[0]
    levels = len(widths) - 1
    width = widths[0]
    rim = lane_up(width - samples + DLOC - 1)
    total = rim + samples
    starts = [width - each for each in widths]
    tiles = width // LANES
    fair = (tiles - 1) // CHUNKS
    most = (widths[-1] // LANES - 1) // max(CHUNKS - 1, 1)
    later = min(fair, most) // 2 * 2 or 1
    sizes = [tiles - later * (CHUNKS - 1)] + [later] * (CHUNKS - 1)
    edges = [LANES * sum(sizes[:count]) for count in range(CHUNKS + 1)]

    def coded():
        return [
            [
                pltpu.VMEM(
                    (rows, edges[c + 1] - max(edges[c], starts[j])),
                    jnp.int16,
                )
                for c in range(CHUNKS)
            ]
            for j in range(levels)
        ]

    tail = lane_up(DLOC * 2 ** (levels - 1) // 2)
    vmem = pl.BlockSpec(memory_space=pltpu.VMEM)
    return pl.pallas_call(
        functools.partial(sweep_kernel, edges, starts, rim),
        name="sweep",
        out_shape=(
            jax.ShapeDtypeStruct((rows, widths[-1]), jnp.float32),
            jax.ShapeDtypeStruct((rows, LANES), jnp.float32),
            jax.ShapeDtypeStruct((box_widths.shape[0], LANES), jnp.int32),
        ),
        in_specs=[pl.BlockSpec(memory_space=pltpu.HBM)] * 6,
        out_specs=(vmem, vmem, vmem),
        scratch_shapes=[
            pltpu.VMEM(delays.shape, jnp.int32),
            pltpu.VMEM(lower_rows.shape, jnp.int32),
            pltpu.VMEM(upper_rows.shape, jnp.int32),
            pltpu.VMEM(level_shifts.shape, jnp.int32),
            pltpu.VMEM((1, box_widths.shape[0]), jnp.int32),
            pltpu.VMEM((channels, LANES + total), jnp.bfloat16),
            pltpu.VMEM((COARSE * rows, FINE * channels), jnp.bfloat16),
            pltpu.VMEM((FINE * channels, 2 * LANES), jnp.bfloat16),
            pltpu.VMEM((COARSE * rows, total), jnp.float32),
            [pltpu.VMEM((rows, width), jnp.float32) for _ in range(levels)],
            [pltpu.VMEM((rows, tail + width), jnp.float32) for _ in range(levels)],
            coded(),
            coded(),
            pltpu.VMEM((levels, CHUNKS, PACKED, LANES), jnp.int16),
            pltpu.VMEM((levels, CHUNKS, PACKED, LANES), jnp.int16),
            pltpu.VMEM((rows, LANES), jnp.float32),
            pltpu.VMEM((rows, LANES), jnp.float32),
            pltpu.SemaphoreType.DMA,
            pltpu.SemaphoreType.DMA((5,)),
            pltpu.SemaphoreType.DMA((2,)),
            pltpu.SemaphoreType.DMA((2,)),
            pltpu.SemaphoreType.DMA((levels, CHUNKS)),
            pltpu.SemaphoreType.DMA((levels, CHUNKS)),
            pltpu.SemaphoreType.DMA((levels, CHUNKS)),
            pltpu.SemaphoreType.DMA((levels, CHUNKS)),
        ],
        compiler_params=pltpu.CompilerParams(
            collective_id=0, has_side_effects=True, vmem_limit_bytes=48 * 2**20
        ),
    )(filterbank, delays, lower_rows, upper_rows, level_shifts, box_widths[None])


def box_kernel(times, widths_ref, state_ref, squares_ref, out_ref, stacked):
    rows = state_ref.shape[0]
    tiles = out_ref.shape[2] // LANES
    per_step = out_ref.shape[0]

    @pl.when(pl.program_id(0) == 0)
    def _():
        for tile in range(tiles):
            part = state_ref[:, tile * LANES : (tile + 2) * LANES]
            high = part.astype(jnp.bfloat16)
            low = (part - high.astype(jnp.float32)).astype(jnp.bfloat16)
            stacked[tile * rows : (tile + 1) * rows, : 2 * LANES] = high
            stacked[tile * rows : (tile + 1) * rows, 2 * LANES :] = low

    inverse = lax.rsqrt(squares_ref[...] / times + 1e-05)
    masks = []
    factors = []
    for which in range(per_step):
        box_width = widths_ref[pl.ds(pl.program_id(0) * per_step + which, 1), :]
        at = lax.broadcasted_iota(jnp.int32, (2 * LANES, LANES), 0) - LANES
        to = lax.broadcasted_iota(jnp.int32, (2 * LANES, LANES), 1)
        inside = (at <= to) & (at > to - box_width)
        mask = jnp.where(inside, 1.0, 0.0).astype(jnp.bfloat16)
        masks.append(jnp.concatenate([mask, mask], axis=0))
        root = jnp.sqrt(box_width.astype(jnp.float32))
        factors.append(inverse / root)
    boxes = jnp.dot(
        stacked[...], jnp.concatenate(masks, axis=1), preferred_element_type=jnp.float32
    )
    for which in range(per_step):
        for tile in range(tiles):
            out_ref[which, :, tile * LANES : (tile + 1) * LANES] = (
                boxes[tile * rows : (tile + 1) * rows, which * LANES : (which + 1) * LANES]
                * factors[which]
            )


def box_filter(widths, state, squares, samples, times):
    rows = state.shape[0]
    count = widths.shape[0]
    per_step = 2 if count % 2 == 0 else 1
    return pl.pallas_call(
        functools.partial(box_kernel, times),
        name="boxes",
        grid=(count // per_step,),
        out_shape=jax.ShapeDtypeStruct((count, rows, samples), jnp.float32),
        in_specs=[
            pl.BlockSpec(memory_space=pltpu.VMEM),
            pl.BlockSpec(memory_space=pltpu.VMEM),
            pl.BlockSpec(memory_space=pltpu.VMEM),
        ],
        out_specs=pl.BlockSpec((per_step, rows, samples), lambda i: (i, 0, 0)),
        scratch_shapes=[pltpu.VMEM((samples // LANES * rows, 4 * LANES), jnp.bfloat16)],
        compiler_params=pltpu.CompilerParams(vmem_limit_bytes=32 * 2**20),
    )(widths, state, squares)


def local(filterbank, local_delays, lower_rows, upper_rows, level_shifts, box_widths):
    samples = filterbank.shape[1]
    levels = lax.axis_size("chan").bit_length() - 1
    needs = [LANES]
    for level in reversed(range(levels)):
        needs.insert(0, needs[0] - (level == levels - 1) + DLOC * 2**level // 2 - 1)
    widths = [samples + lane_up(need + 1) for need in needs[:-1]] + [samples + LANES]
    state, squares, spans = sweep(
        filterbank, local_delays.T, lower_rows, upper_rows, level_shifts, box_widths, widths
    )
    return box_filter(spans, state, squares, samples, samples * lax.axis_size("tm"))


def solution(mesh):
    placed = (
        P(("beam", "chan"), "tm"),
        P("chan", None),
        P(None, "chan"),
        P(None, "chan"),
        P(None, "chan"),
        P(),
    )
    return jax.shard_map(
        local,
        mesh=mesh,
        in_specs=placed,
        out_specs=P(None, ("beam", "chan"), "tm"),
        check_vma=False,
    )
```

```python
import functools

import jax
import jax.numpy as jnp
from jax import lax
from jax.experimental import pallas as pl
from jax.experimental.pallas import tpu as pltpu
from jax.sharding import PartitionSpec as P

DLOC = 64
LANES = 128
FINE = 8
COARSE = DLOC // FINE
CHUNKS = 3
PACKED = 16
MESH = pl.DeviceIdType.MESH


def lane_up(count):
    return -(-count // LANES) * LANES


def code_rows(rows):
    largest = jnp.maximum(jnp.max(jnp.abs(rows), axis=1, keepdims=True), 2.0**-100)
    exponent = jnp.floor(jnp.log2(largest))
    coded = jnp.round(jnp.clip(rows * jnp.exp2(14.0 - exponent), -32767.0, 32767.0))
    at = lax.broadcasted_iota(jnp.int32, (rows.shape[0], LANES), 0)
    to = lax.broadcasted_iota(jnp.int32, (rows.shape[0], LANES), 1)
    along = jnp.sum(jnp.where(at == to, exponent, 0.0), axis=0, keepdims=True)
    along = jnp.broadcast_to(along, (PACKED, LANES))
    return coded.astype(jnp.int32).astype(jnp.int16), along.astype(jnp.int32).astype(jnp.int16)


def decode_rows(coded, along):
    values = coded.astype(jnp.int32).astype(jnp.float32)
    exponents = along.astype(jnp.int32)[:1, : coded.shape[0]]
    return values * jnp.exp2(as_column(exponents).astype(jnp.float32) - 14.0)


def as_column(row):
    count = row.shape[1]
    at = lax.broadcasted_iota(jnp.int32, (count, count), 0)
    to = lax.broadcasted_iota(jnp.int32, (count, count), 1)
    spread = jnp.where(at == to, row.astype(jnp.float32), 0.0)
    return jnp.sum(spread, axis=1, keepdims=True).astype(jnp.int32)


def pick(index, source):
    rows = source.shape[0]
    at = lax.broadcasted_iota(jnp.int32, (index.shape[0], rows), 1)
    once = jnp.where(at == index, 1.0, 0.0).astype(jnp.bfloat16)
    chosen = jnp.concatenate([once, once], axis=1)
    high = source.astype(jnp.bfloat16)
    low = (source - high.astype(jnp.float32)).astype(jnp.bfloat16)
    return jnp.dot(
        chosen, jnp.concatenate([high, low], axis=0), preferred_element_type=jnp.float32
    )


def sweep_kernel(
    edges,
    starts,
    rim,
    fb_ref,
    delays_hbm,
    lower_hbm,
    upper_hbm,
    shifts_hbm,
    widths_hbm,
    state_ref,
    squares_ref,
    widths_ref,
    delays_ref,
    lower_ref,
    upper_ref,
    shifts_ref,
    widths_row,
    ext,
    onehot,
    spread,
    partial,
    owns,
    picked,
    outgoing,
    incoming,
    scale_out,
    scale_in,
    square_out,
    square_in,
    local_sem,
    small_sem,
    pair_send,
    pair_recv,
    send_sem,
    recv_sem,
    scale_send,
    scale_recv,
):
    channels, samples = fb_ref.shape
    rows = delays_ref.shape[0]
    levels = len(owns)
    chunks = len(edges) - 1
    width = edges[-1]
    total = rim + samples
    skip = total - width
    tail = picked[0].shape[1] - width
    sent_rim = min(rim, samples)
    empty = LANES + rim - sent_rim

    chan = lax.axis_index("chan")
    tm = lax.axis_index("tm")
    sides = [lax.rem(lax.div(chan, 1 << level), 2) for level in range(levels)]
    partners = [
        {"chan": chan + (1 << level) - (2 << level) * sides[level]} for level in range(levels)
    ]
    pair = {"tm": 1 - tm}

    barrier = pltpu.get_barrier_semaphore()
    for device in [pair] + partners:
        pl.semaphore_signal(barrier, inc=1, device_id=device, device_id_type=MESH)
    own_copy = pltpu.make_async_copy(fb_ref, ext.at[:, pl.ds(LANES + rim, samples)], local_sem)
    small_copies = [
        pltpu.make_async_copy(source, target, small_sem.at[at])
        for at, (source, target) in enumerate(
            [
                (delays_hbm, delays_ref),
                (lower_hbm, lower_ref),
                (upper_hbm, upper_ref),
                (shifts_hbm, shifts_ref),
                (widths_hbm, widths_row),
            ]
        )
    ]
    for copy in small_copies:
        copy.start()
    own_copy.start()
    pl.semaphore_wait(barrier, levels + 1)
    rim_copy = pltpu.make_async_remote_copy(
        src_ref=fb_ref.at[:, pl.ds(samples - sent_rim, sent_rim)],
        dst_ref=ext.at[:, pl.ds(empty, sent_rim)],
        send_sem=pair_send.at[0],
        recv_sem=pair_recv.at[0],
        device_id=pair,
        device_id_type=MESH,
    )
    rim_copy.start()

    ext[:, :empty] = jnp.zeros((channels, empty), jnp.bfloat16)
    for level in range(levels):
        picked[level][:, :tail] = jnp.zeros((rows, tail), jnp.float32)
    for copy in small_copies:
        copy.wait()
    widths_ref[...] = jnp.broadcast_to(as_column(widths_row[...]), widths_ref.shape)
    for coarse in range(COARSE):
        relative = delays_ref[...] - FINE * coarse
        for fine in range(FINE):
            onehot[coarse * rows : (coarse + 1) * rows, fine * channels : (fine + 1) * channels] = (
                jnp.where(relative == fine, 1.0, 0.0).astype(jnp.bfloat16)
            )
    lows = [as_column(lower_ref[level : level + 1, :]) for level in range(levels)]
    highs = [as_column(upper_ref[level : level + 1, :]) for level in range(levels)]
    shifts = [as_column(shifts_ref[level : level + 1, :]) for level in range(levels)]

    def first_of(level, chunk):
        return max(edges[chunk], starts[level])

    def history(level, chunk):
        begin = first_of(level, chunk)
        return min(max(width - samples - begin, 0), edges[chunk + 1] - begin)

    def exchange(level, chunk, act):
        old = history(level, chunk)
        size = edges[chunk + 1] - first_of(level, chunk)

        def columns(begin):
            act(
                pltpu.make_async_remote_copy(
                    src_ref=outgoing[level][chunk].at[:, pl.ds(begin, size - begin)],
                    dst_ref=incoming[level][chunk].at[:, pl.ds(begin, size - begin)],
                    send_sem=send_sem.at[level, chunk],
                    recv_sem=recv_sem.at[level, chunk],
                    device_id=partners[level],
                    device_id_type=MESH,
                )
            )

        act(
            pltpu.make_async_remote_copy(
                src_ref=scale_out.at[level, chunk],
                dst_ref=scale_in.at[level, chunk],
                send_sem=scale_send.at[level, chunk],
                recv_sem=scale_recv.at[level, chunk],
                device_id=partners[level],
                device_id_type=MESH,
            )
        )
        if old:
            pl.when(tm > 0)(lambda: columns(0))
            if old < size:
                pl.when(tm == 0)(lambda: columns(old))
        else:
            columns(0)

    def hand_on(level, chunk, values):
        owns[level][:, first_of(level, chunk) : edges[chunk + 1]] = values
        outgoing[level][chunk][...], scale_out[level, chunk] = code_rows(values)
        exchange(level, chunk, lambda copy: copy.start())

    @pl.when(tm == 0)
    def _():
        for level in range(levels):
            for chunk in range(chunks):
                old = history(level, chunk)
                if old:
                    incoming[level][chunk][:, :old] = jnp.zeros((rows, old), jnp.int16)

    def dedisperse(chunk):
        begin = skip + edges[chunk] if chunk else 0
        end = skip + edges[chunk + 1]
        tile = 2 * LANES if (end - begin) % (2 * LANES) == 0 else LANES

        def step(index, carry):
            start = pl.multiple_of(begin + index * tile, LANES)
            window = ext[:, pl.ds(start, tile + LANES)]
            for fine in range(FINE):
                spread[fine * channels : (fine + 1) * channels, :tile] = window[
                    :, LANES - fine : LANES - fine + tile
                ]
            partial[:, pl.ds(start, tile)] = jnp.dot(
                onehot[...], spread[:, :tile], preferred_element_type=jnp.float32
            )
            return carry

        lax.fori_loop(0, (end - begin) // tile, step, 0)
        summed = None
        for coarse in range(COARSE):
            back = skip - FINE * coarse
            term = partial[
                coarse * rows : (coarse + 1) * rows, back + edges[chunk] : back + edges[chunk + 1]
            ]
            summed = term if summed is None else summed + term
        hand_on(0, chunk, summed)

    def merge(level, chunk):
        begin, end = first_of(level, chunk), edges[chunk + 1]
        exchange(level, chunk, lambda copy: copy.wait_recv())
        own = owns[level][:, begin:end]
        partner = decode_rows(incoming[level][chunk][...], scale_in[level, chunk])
        upper_side = sides[level] == 1
        low = pick(lows[level], jnp.where(upper_side, partner, own))
        high = pick(highs[level], jnp.where(upper_side, own, partner))
        reach = DLOC * 2**level // 2
        room = lane_up(reach)
        picked[level][:, tail + begin : tail + end] = high
        moved = picked[level][:, tail + begin - room : tail + end]
        for bit in range((reach - 1).bit_length()):
            moved = jnp.where(
                (shifts[level] >> bit) & 1 == 1, pltpu.roll(moved, 2**bit, 1), moved
            )
        after = max(edges[chunk], starts[level + 1])
        return (low + moved[:, room:])[:, after - begin :]

    own_copy.wait()
    rim_copy.wait()
    ext[:, empty : LANES + rim] = jnp.where(
        tm == 0, jnp.zeros((channels, sent_rim), jnp.bfloat16), ext[:, empty : LANES + rim]
    )
    squares = jnp.zeros((rows, 1), jnp.float32)
    for turn in range(chunks + levels):
        if turn < chunks:
            dedisperse(turn)
        for level in range(levels):
            chunk = turn - 1 - level
            if not 0 <= chunk < chunks:
                continue
            merged = merge(level, chunk)
            if level < levels - 1:
                hand_on(level + 1, chunk, merged)
            else:
                begin = first_of(levels, chunk)
                state_ref[:, begin - starts[levels] : edges[chunk + 1] - starts[levels]] = merged
                if edges[chunk + 1] > width - samples:
                    fresh = merged[:, max(width - samples - begin, 0) :]
                    squares = squares + jnp.sum(fresh * fresh, axis=1, keepdims=True)
    square_out[...] = jnp.broadcast_to(squares, (rows, LANES))
    square_copy = pltpu.make_async_remote_copy(
        src_ref=square_out,
        dst_ref=square_in,
        send_sem=pair_send.at[1],
        recv_sem=pair_recv.at[1],
        device_id=pair,
        device_id_type=MESH,
    )
    square_copy.start()
    for level in range(levels):
        for chunk in range(chunks):
            exchange(level, chunk, lambda copy: copy.wait_send())
    square_copy.wait()
    squares_ref[...] = square_out[...] + square_in[...]


def sweep(filterbank, delays, lower_rows, upper_rows, level_shifts, box_widths, widths):
    channels, samples = filterbank.shape
    rows = delays.shape[0]
    levels = len(widths) - 1
    width = widths[0]
    rim = lane_up(width - samples + DLOC - 1)
    total = rim + samples
    starts = [width - each for each in widths]
    tiles = width // LANES
    fair = (tiles - 1) // CHUNKS
    most = (widths[-1] // LANES - 1) // max(CHUNKS - 1, 1)
    later = min(fair, most) // 2 * 2 or 1
    sizes = [tiles - later * (CHUNKS - 1)] + [later] * (CHUNKS - 1)
    edges = [LANES * sum(sizes[:count]) for count in range(CHUNKS + 1)]

    def coded():
        return [
            [
                pltpu.VMEM(
                    (rows, edges[c + 1] - max(edges[c], starts[j])),
                    jnp.int16,
                )
                for c in range(CHUNKS)
            ]
            for j in range(levels)
        ]

    tail = lane_up(DLOC * 2 ** (levels - 1) // 2)
    vmem = pl.BlockSpec(memory_space=pltpu.VMEM)
    return pl.pallas_call(
        functools.partial(sweep_kernel, edges, starts, rim),
        name="sweep",
        out_shape=(
            jax.ShapeDtypeStruct((rows, widths[-1]), jnp.float32),
            jax.ShapeDtypeStruct((rows, LANES), jnp.float32),
            jax.ShapeDtypeStruct((box_widths.shape[0], LANES), jnp.int32),
        ),
        in_specs=[pl.BlockSpec(memory_space=pltpu.HBM)] * 6,
        out_specs=(vmem, vmem, vmem),
        scratch_shapes=[
            pltpu.VMEM(delays.shape, jnp.int32),
            pltpu.VMEM(lower_rows.shape, jnp.int32),
            pltpu.VMEM(upper_rows.shape, jnp.int32),
            pltpu.VMEM(level_shifts.shape, jnp.int32),
            pltpu.VMEM((1, box_widths.shape[0]), jnp.int32),
            pltpu.VMEM((channels, LANES + total), jnp.bfloat16),
            pltpu.VMEM((COARSE * rows, FINE * channels), jnp.bfloat16),
            pltpu.VMEM((FINE * channels, 2 * LANES), jnp.bfloat16),
            pltpu.VMEM((COARSE * rows, total), jnp.float32),
            [pltpu.VMEM((rows, width), jnp.float32) for _ in range(levels)],
            [pltpu.VMEM((rows, tail + width), jnp.float32) for _ in range(levels)],
            coded(),
            coded(),
            pltpu.VMEM((levels, CHUNKS, PACKED, LANES), jnp.int16),
            pltpu.VMEM((levels, CHUNKS, PACKED, LANES), jnp.int16),
            pltpu.VMEM((rows, LANES), jnp.float32),
            pltpu.VMEM((rows, LANES), jnp.float32),
            pltpu.SemaphoreType.DMA,
            pltpu.SemaphoreType.DMA((5,)),
            pltpu.SemaphoreType.DMA((2,)),
            pltpu.SemaphoreType.DMA((2,)),
            pltpu.SemaphoreType.DMA((levels, CHUNKS)),
            pltpu.SemaphoreType.DMA((levels, CHUNKS)),
            pltpu.SemaphoreType.DMA((levels, CHUNKS)),
            pltpu.SemaphoreType.DMA((levels, CHUNKS)),
        ],
        compiler_params=pltpu.CompilerParams(
            collective_id=0, has_side_effects=True, vmem_limit_bytes=48 * 2**20
        ),
    )(
        *[
            pltpu.with_memory_space_constraint(each, pltpu.HBM)
            for each in (filterbank, delays, lower_rows, upper_rows, level_shifts, box_widths[None])
        ]
    )


def box_kernel(times, widths_ref, state_ref, squares_ref, out_ref, stacked):
    rows = state_ref.shape[0]
    tiles = out_ref.shape[2] // LANES
    per_step = out_ref.shape[0]

    @pl.when(pl.program_id(0) == 0)
    def _():
        for tile in range(tiles):
            part = state_ref[:, tile * LANES : (tile + 2) * LANES]
            high = part.astype(jnp.bfloat16)
            low = (part - high.astype(jnp.float32)).astype(jnp.bfloat16)
            stacked[tile * rows : (tile + 1) * rows, : 2 * LANES] = high
            stacked[tile * rows : (tile + 1) * rows, 2 * LANES :] = low

    inverse = lax.rsqrt(squares_ref[...] / times + 1e-05)
    masks = []
    factors = []
    for which in range(per_step):
        box_width = widths_ref[pl.ds(pl.program_id(0) * per_step + which, 1), :]
        at = lax.broadcasted_iota(jnp.int32, (2 * LANES, LANES), 0) - LANES
        to = lax.broadcasted_iota(jnp.int32, (2 * LANES, LANES), 1)
        inside = (at <= to) & (at > to - box_width)
        mask = jnp.where(inside, 1.0, 0.0).astype(jnp.bfloat16)
        masks.append(jnp.concatenate([mask, mask], axis=0))
        root = jnp.sqrt(box_width.astype(jnp.float32))
        factors.append(inverse / root)
    boxes = jnp.dot(
        stacked[...], jnp.concatenate(masks, axis=1), preferred_element_type=jnp.float32
    )
    for which in range(per_step):
        for tile in range(tiles):
            out_ref[which, :, tile * LANES : (tile + 1) * LANES] = (
                boxes[tile * rows : (tile + 1) * rows, which * LANES : (which + 1) * LANES]
                * factors[which]
            )


def box_filter(widths, state, squares, samples, times):
    rows = state.shape[0]
    count = widths.shape[0]
    per_step = 2 if count % 2 == 0 else 1
    return pl.pallas_call(
        functools.partial(box_kernel, times),
        name="boxes",
        grid=(count // per_step,),
        out_shape=jax.ShapeDtypeStruct((count, rows, samples), jnp.float32),
        in_specs=[
            pl.BlockSpec(memory_space=pltpu.VMEM),
            pl.BlockSpec(memory_space=pltpu.VMEM),
            pl.BlockSpec(memory_space=pltpu.VMEM),
        ],
        out_specs=pl.BlockSpec((per_step, rows, samples), lambda i: (i, 0, 0)),
        scratch_shapes=[pltpu.VMEM((samples // LANES * rows, 4 * LANES), jnp.bfloat16)],
        compiler_params=pltpu.CompilerParams(vmem_limit_bytes=32 * 2**20),
    )(widths, state, squares)


def local(filterbank, local_delays, lower_rows, upper_rows, level_shifts, box_widths):
    samples = filterbank.shape[1]
    levels = lax.axis_size("chan").bit_length() - 1
    needs = [LANES]
    for level in reversed(range(levels)):
        needs.insert(0, needs[0] - (level == levels - 1) + DLOC * 2**level // 2 - 1)
    widths = [samples + lane_up(need + 1) for need in needs[:-1]] + [samples + LANES]
    state, squares, spans = sweep(
        filterbank, local_delays.T, lower_rows, upper_rows, level_shifts, box_widths, widths
    )
    return box_filter(spans, state, squares, samples, samples * lax.axis_size("tm"))


def solution(mesh):
    placed = (
        P(("beam", "chan"), "tm"),
        P("chan", None),
        P(None, "chan"),
        P(None, "chan"),
        P(None, "chan"),
        P(),
    )
    return jax.shard_map(
        local,
        mesh=mesh,
        in_specs=placed,
        out_specs=P(None, ("beam", "chan"), "tm"),
        check_vma=False,
    )
```

```python
import functools

import jax
import jax.numpy as jnp
from jax import lax
from jax.experimental import pallas as pl
from jax.experimental.pallas import tpu as pltpu
from jax.sharding import PartitionSpec as P

DLOC = 64
LANES = 128
FINE = 8
COARSE = DLOC // FINE
CHUNKS = 3
PACKED = 16
TILES = (1024, 768, 512, 256, 128)
MESH = pl.DeviceIdType.MESH


def lane_up(count):
    return -(-count // LANES) * LANES


def code_rows(rows):
    largest = jnp.maximum(jnp.max(jnp.abs(rows), axis=1, keepdims=True), 2.0**-100)
    exponent = jnp.floor(jnp.log2(largest))
    coded = jnp.round(jnp.clip(rows * jnp.exp2(14.0 - exponent), -32767.0, 32767.0))
    at = lax.broadcasted_iota(jnp.int32, (rows.shape[0], LANES), 0)
    to = lax.broadcasted_iota(jnp.int32, (rows.shape[0], LANES), 1)
    along = jnp.sum(jnp.where(at == to, exponent, 0.0), axis=0, keepdims=True)
    along = jnp.broadcast_to(along, (PACKED, LANES))
    return coded.astype(jnp.int32).astype(jnp.int16), along.astype(jnp.int32).astype(jnp.int16)


def decode_rows(coded, along):
    values = coded.astype(jnp.int32).astype(jnp.float32)
    exponents = along.astype(jnp.int32)[:1, : coded.shape[0]]
    return values * jnp.exp2(as_column(exponents).astype(jnp.float32) - 14.0)


def as_column(row):
    count = row.shape[1]
    at = lax.broadcasted_iota(jnp.int32, (count, count), 0)
    to = lax.broadcasted_iota(jnp.int32, (count, count), 1)
    spread = jnp.where(at == to, row.astype(jnp.float32), 0.0)
    return jnp.sum(spread, axis=1, keepdims=True).astype(jnp.int32)


def pick(index, source):
    rows = source.shape[0]
    at = lax.broadcasted_iota(jnp.int32, (index.shape[0], rows), 1)
    once = jnp.where(at == index, 1.0, 0.0).astype(jnp.bfloat16)
    chosen = jnp.concatenate([once, once], axis=1)
    high = source.astype(jnp.bfloat16)
    low = (source - high.astype(jnp.float32)).astype(jnp.bfloat16)
    return jnp.dot(
        chosen, jnp.concatenate([high, low], axis=0), preferred_element_type=jnp.float32
    )


def sweep_kernel(
    edges,
    starts,
    rim,
    fb_ref,
    delays_hbm,
    lower_hbm,
    upper_hbm,
    shifts_hbm,
    widths_hbm,
    state_ref,
    squares_ref,
    widths_ref,
    delays_ref,
    lower_ref,
    upper_ref,
    shifts_ref,
    widths_row,
    ext,
    onehot,
    spread,
    partial,
    owns,
    picked,
    outgoing,
    incoming,
    scale_out,
    scale_in,
    square_out,
    square_in,
    local_sem,
    small_sem,
    pair_send,
    pair_recv,
    send_sem,
    recv_sem,
    scale_send,
    scale_recv,
):
    channels, samples = fb_ref.shape
    rows = delays_ref.shape[0]
    levels = len(owns)
    chunks = len(edges) - 1
    width = edges[-1]
    total = rim + samples
    skip = total - width
    tail = picked[0].shape[1] - width
    sent_rim = min(rim, samples)
    empty = LANES + rim - sent_rim

    chan = lax.axis_index("chan")
    tm = lax.axis_index("tm")
    sides = [lax.rem(lax.div(chan, 1 << level), 2) for level in range(levels)]
    partners = [
        {"chan": chan + (1 << level) - (2 << level) * sides[level]} for level in range(levels)
    ]
    pair = {"tm": 1 - tm}

    barrier = pltpu.get_barrier_semaphore()
    for device in [pair] + partners:
        pl.semaphore_signal(barrier, inc=1, device_id=device, device_id_type=MESH)
    own_copy = pltpu.make_async_copy(fb_ref, ext.at[:, pl.ds(LANES + rim, samples)], local_sem)
    small_copies = [
        pltpu.make_async_copy(source, target, small_sem.at[at])
        for at, (source, target) in enumerate(
            [
                (delays_hbm, delays_ref),
                (lower_hbm, lower_ref),
                (upper_hbm, upper_ref),
                (shifts_hbm, shifts_ref),
                (widths_hbm, widths_row),
            ]
        )
    ]
    for copy in small_copies:
        copy.start()
    own_copy.start()
    pl.semaphore_wait(barrier, levels + 1)
    rim_copy = pltpu.make_async_remote_copy(
        src_ref=fb_ref.at[:, pl.ds(samples - sent_rim, sent_rim)],
        dst_ref=ext.at[:, pl.ds(empty, sent_rim)],
        send_sem=pair_send.at[0],
        recv_sem=pair_recv.at[0],
        device_id=pair,
        device_id_type=MESH,
    )
    rim_copy.start()

    ext[:, :empty] = jnp.zeros((channels, empty), jnp.bfloat16)
    for level in range(levels):
        picked[level][:, :tail] = jnp.zeros((rows, tail), jnp.float32)
    for copy in small_copies:
        copy.wait()
    widths_ref[...] = jnp.broadcast_to(as_column(widths_row[...]), widths_ref.shape)
    for coarse in range(COARSE):
        relative = delays_ref[...] - FINE * coarse
        for fine in range(FINE):
            onehot[coarse * rows : (coarse + 1) * rows, fine * channels : (fine + 1) * channels] = (
                jnp.where(relative == fine, 1.0, 0.0).astype(jnp.bfloat16)
            )
    lows = [as_column(lower_ref[level : level + 1, :]) for level in range(levels)]
    highs = [as_column(upper_ref[level : level + 1, :]) for level in range(levels)]
    shifts = [as_column(shifts_ref[level : level + 1, :]) for level in range(levels)]

    def first_of(level, chunk):
        return max(edges[chunk], starts[level])

    def history(level, chunk):
        begin = first_of(level, chunk)
        return min(max(width - samples - begin, 0), edges[chunk + 1] - begin)

    def exchange(level, chunk, act):
        old = history(level, chunk)
        size = edges[chunk + 1] - first_of(level, chunk)

        def columns(begin):
            act(
                pltpu.make_async_remote_copy(
                    src_ref=outgoing[level][chunk].at[:, pl.ds(begin, size - begin)],
                    dst_ref=incoming[level][chunk].at[:, pl.ds(begin, size - begin)],
                    send_sem=send_sem.at[level, chunk],
                    recv_sem=recv_sem.at[level, chunk],
                    device_id=partners[level],
                    device_id_type=MESH,
                )
            )

        act(
            pltpu.make_async_remote_copy(
                src_ref=scale_out.at[level, chunk],
                dst_ref=scale_in.at[level, chunk],
                send_sem=scale_send.at[level, chunk],
                recv_sem=scale_recv.at[level, chunk],
                device_id=partners[level],
                device_id_type=MESH,
            )
        )
        if old:
            pl.when(tm > 0)(lambda: columns(0))
            if old < size:
                pl.when(tm == 0)(lambda: columns(old))
        else:
            columns(0)

    def hand_on(level, chunk, values):
        owns[level][:, first_of(level, chunk) : edges[chunk + 1]] = values
        outgoing[level][chunk][...], scale_out[level, chunk] = code_rows(values)
        exchange(level, chunk, lambda copy: copy.start())

    @pl.when(tm == 0)
    def _():
        for level in range(levels):
            for chunk in range(chunks):
                old = history(level, chunk)
                if old:
                    incoming[level][chunk][:, :old] = jnp.zeros((rows, old), jnp.int16)

    def dedisperse(chunk):
        begin = skip + edges[chunk] if chunk else 0
        end = skip + edges[chunk + 1]
        tile = next(t for t in TILES if (end - begin) % t == 0)

        def step(index, carry):
            start = pl.multiple_of(begin + index * tile, LANES)
            window = ext[:, pl.ds(start, tile + LANES)]
            for fine in range(FINE):
                spread[fine * channels : (fine + 1) * channels, :tile] = window[
                    :, LANES - fine : LANES - fine + tile
                ]
            partial[:, pl.ds(start, tile)] = jnp.dot(
                onehot[...], spread[:, :tile], preferred_element_type=jnp.float32
            )
            return carry

        lax.fori_loop(0, (end - begin) // tile, step, 0)
        summed = None
        for coarse in range(COARSE):
            back = skip - FINE * coarse
            term = partial[
                coarse * rows : (coarse + 1) * rows, back + edges[chunk] : back + edges[chunk + 1]
            ]
            summed = term if summed is None else summed + term
        hand_on(0, chunk, summed)

    def merge(level, chunk):
        begin, end = first_of(level, chunk), edges[chunk + 1]
        exchange(level, chunk, lambda copy: copy.wait_recv())
        own = owns[level][:, begin:end]
        partner = decode_rows(incoming[level][chunk][...], scale_in[level, chunk])
        upper_side = sides[level] == 1
        low = pick(lows[level], jnp.where(upper_side, partner, own))
        high = pick(highs[level], jnp.where(upper_side, own, partner))
        reach = DLOC * 2**level // 2
        room = lane_up(reach)
        picked[level][:, tail + begin : tail + end] = high
        moved = picked[level][:, tail + begin - room : tail + end]
        for bit in range((reach - 1).bit_length()):
            moved = jnp.where(
                (shifts[level] >> bit) & 1 == 1, pltpu.roll(moved, 2**bit, 1), moved
            )
        after = max(edges[chunk], starts[level + 1])
        return (low + moved[:, room:])[:, after - begin :]

    own_copy.wait()
    rim_copy.wait()
    ext[:, empty : LANES + rim] = jnp.where(
        tm == 0, jnp.zeros((channels, sent_rim), jnp.bfloat16), ext[:, empty : LANES + rim]
    )
    squares = jnp.zeros((rows, 1), jnp.float32)
    for turn in range(chunks + levels):
        if turn < chunks:
            dedisperse(turn)
        for level in range(levels):
            chunk = turn - 1 - level
            if not 0 <= chunk < chunks:
                continue
            merged = merge(level, chunk)
            if level < levels - 1:
                hand_on(level + 1, chunk, merged)
            else:
                begin = first_of(levels, chunk)
                state_ref[:, begin - starts[levels] : edges[chunk + 1] - starts[levels]] = merged
                if edges[chunk + 1] > width - samples:
                    fresh = merged[:, max(width - samples - begin, 0) :]
                    squares = squares + jnp.sum(fresh * fresh, axis=1, keepdims=True)
    square_out[...] = jnp.broadcast_to(squares, (rows, LANES))
    square_copy = pltpu.make_async_remote_copy(
        src_ref=square_out,
        dst_ref=square_in,
        send_sem=pair_send.at[1],
        recv_sem=pair_recv.at[1],
        device_id=pair,
        device_id_type=MESH,
    )
    square_copy.start()
    for level in range(levels):
        for chunk in range(chunks):
            exchange(level, chunk, lambda copy: copy.wait_send())
    square_copy.wait()
    squares_ref[...] = square_out[...] + square_in[...]


def sweep(filterbank, delays, lower_rows, upper_rows, level_shifts, box_widths, widths):
    channels, samples = filterbank.shape
    rows = delays.shape[0]
    levels = len(widths) - 1
    width = widths[0]
    rim = lane_up(width - samples + DLOC - 1)
    total = rim + samples
    starts = [width - each for each in widths]
    tiles = width // LANES
    fair = (tiles - 1) // CHUNKS
    most = (widths[-1] // LANES - 1) // max(CHUNKS - 1, 1)
    later = min(fair, most) // 2 * 2 or 1
    sizes = [tiles - later * (CHUNKS - 1)] + [later] * (CHUNKS - 1)
    edges = [LANES * sum(sizes[:count]) for count in range(CHUNKS + 1)]

    def coded():
        return [
            [
                pltpu.VMEM(
                    (rows, edges[c + 1] - max(edges[c], starts[j])),
                    jnp.int16,
                )
                for c in range(CHUNKS)
            ]
            for j in range(levels)
        ]

    tail = lane_up(DLOC * 2 ** (levels - 1) // 2)
    vmem = pl.BlockSpec(memory_space=pltpu.VMEM)
    return pl.pallas_call(
        functools.partial(sweep_kernel, edges, starts, rim),
        name="sweep",
        out_shape=(
            jax.ShapeDtypeStruct((rows, widths[-1]), jnp.float32),
            jax.ShapeDtypeStruct((rows, LANES), jnp.float32),
            jax.ShapeDtypeStruct((box_widths.shape[0], LANES), jnp.int32),
        ),
        in_specs=[pl.BlockSpec(memory_space=pltpu.HBM)] * 6,
        out_specs=(vmem, vmem, vmem),
        scratch_shapes=[
            pltpu.VMEM(delays.shape, jnp.int32),
            pltpu.VMEM(lower_rows.shape, jnp.int32),
            pltpu.VMEM(upper_rows.shape, jnp.int32),
            pltpu.VMEM(level_shifts.shape, jnp.int32),
            pltpu.VMEM((1, box_widths.shape[0]), jnp.int32),
            pltpu.VMEM((channels, LANES + total), jnp.bfloat16),
            pltpu.VMEM((COARSE * rows, FINE * channels), jnp.bfloat16),
            pltpu.VMEM((FINE * channels, TILES[0]), jnp.bfloat16),
            pltpu.VMEM((COARSE * rows, total), jnp.float32),
            [pltpu.VMEM((rows, width), jnp.float32) for _ in range(levels)],
            [pltpu.VMEM((rows, tail + width), jnp.float32) for _ in range(levels)],
            coded(),
            coded(),
            pltpu.VMEM((levels, CHUNKS, PACKED, LANES), jnp.int16),
            pltpu.VMEM((levels, CHUNKS, PACKED, LANES), jnp.int16),
            pltpu.VMEM((rows, LANES), jnp.float32),
            pltpu.VMEM((rows, LANES), jnp.float32),
            pltpu.SemaphoreType.DMA,
            pltpu.SemaphoreType.DMA((5,)),
            pltpu.SemaphoreType.DMA((2,)),
            pltpu.SemaphoreType.DMA((2,)),
            pltpu.SemaphoreType.DMA((levels, CHUNKS)),
            pltpu.SemaphoreType.DMA((levels, CHUNKS)),
            pltpu.SemaphoreType.DMA((levels, CHUNKS)),
            pltpu.SemaphoreType.DMA((levels, CHUNKS)),
        ],
        compiler_params=pltpu.CompilerParams(
            collective_id=0, has_side_effects=True, vmem_limit_bytes=48 * 2**20
        ),
    )(
        *[
            pltpu.with_memory_space_constraint(each, pltpu.HBM)
            for each in (filterbank, delays, lower_rows, upper_rows, level_shifts, box_widths[None])
        ]
    )


def box_kernel(times, widths_ref, state_ref, squares_ref, out_ref, stacked):
    rows = state_ref.shape[0]
    tiles = out_ref.shape[2] // LANES
    per_step = out_ref.shape[0]

    @pl.when(pl.program_id(0) == 0)
    def _():
        for tile in range(tiles):
            part = state_ref[:, tile * LANES : (tile + 2) * LANES]
            high = part.astype(jnp.bfloat16)
            low = (part - high.astype(jnp.float32)).astype(jnp.bfloat16)
            stacked[tile * rows : (tile + 1) * rows, : 2 * LANES] = high
            stacked[tile * rows : (tile + 1) * rows, 2 * LANES :] = low

    inverse = lax.rsqrt(squares_ref[...] / times + 1e-05)
    masks = []
    factors = []
    for which in range(per_step):
        box_width = widths_ref[pl.ds(pl.program_id(0) * per_step + which, 1), :]
        at = lax.broadcasted_iota(jnp.int32, (2 * LANES, LANES), 0) - LANES
        to = lax.broadcasted_iota(jnp.int32, (2 * LANES, LANES), 1)
        inside = (at <= to) & (at > to - box_width)
        mask = jnp.where(inside, 1.0, 0.0).astype(jnp.bfloat16)
        masks.append(jnp.concatenate([mask, mask], axis=0))
        root = jnp.sqrt(box_width.astype(jnp.float32))
        factors.append(inverse / root)
    boxes = jnp.dot(
        stacked[...], jnp.concatenate(masks, axis=1), preferred_element_type=jnp.float32
    )
    for which in range(per_step):
        for tile in range(tiles):
            out_ref[which, :, tile * LANES : (tile + 1) * LANES] = (
                boxes[tile * rows : (tile + 1) * rows, which * LANES : (which + 1) * LANES]
                * factors[which]
            )


def box_filter(widths, state, squares, samples, times):
    rows = state.shape[0]
    count = widths.shape[0]
    per_step = 2 if count % 2 == 0 else 1
    return pl.pallas_call(
        functools.partial(box_kernel, times),
        name="boxes",
        grid=(count // per_step,),
        out_shape=jax.ShapeDtypeStruct((count, rows, samples), jnp.float32),
        in_specs=[
            pl.BlockSpec(memory_space=pltpu.VMEM),
            pl.BlockSpec(memory_space=pltpu.VMEM),
            pl.BlockSpec(memory_space=pltpu.VMEM),
        ],
        out_specs=pl.BlockSpec((per_step, rows, samples), lambda i: (i, 0, 0)),
        scratch_shapes=[pltpu.VMEM((samples // LANES * rows, 4 * LANES), jnp.bfloat16)],
        compiler_params=pltpu.CompilerParams(vmem_limit_bytes=32 * 2**20),
    )(widths, state, squares)


def local(filterbank, local_delays, lower_rows, upper_rows, level_shifts, box_widths):
    samples = filterbank.shape[1]
    levels = lax.axis_size("chan").bit_length() - 1
    needs = [LANES]
    for level in reversed(range(levels)):
        needs.insert(0, needs[0] - (level == levels - 1) + DLOC * 2**level // 2 - 1)
    widths = [samples + lane_up(need + 1) for need in needs[:-1]] + [samples + LANES]
    state, squares, spans = sweep(
        filterbank, local_delays.T, lower_rows, upper_rows, level_shifts, box_widths, widths
    )
    return box_filter(spans, state, squares, samples, samples * lax.axis_size("tm"))


def solution(mesh):
    placed = (
        P(("beam", "chan"), "tm"),
        P("chan", None),
        P(None, "chan"),
        P(None, "chan"),
        P(None, "chan"),
        P(),
    )
    return jax.shard_map(
        local,
        mesh=mesh,
        in_specs=placed,
        out_specs=P(None, ("beam", "chan"), "tm"),
        check_vma=False,
    )
```
